32 devices in a mesh: dp: 8 (over z, x), head: 4 (over y, core).
Axes of the slice: x: 2, y: 2, z: 4, core: 2. Of those that a mesh axis runs over, the one named last changes fastest.
Arguments:
- residual: bfloat16 [32, 4096], P('dp', 'head'), may hold values from -6 to 6
- query: bfloat16 [32, 32, 128], P('dp', 'head'), may hold values from -4.5 to 4.5
- fresh_token_keys: bfloat16 [32, 8, 128], P('dp', 'head'), may hold values from -4.5 to 4.5
- value_new: bfloat16 [32, 8, 128], P('dp', 'head'), may hold values from -24 to 24
- key_cache: bfloat16 [32, 8, 2048, 128], P('dp', 'head'), may hold values from -6 to 6
- value_cache: bfloat16 [32, 8, 2048, 128], P('dp', 'head'), may hold values from -6 to 6
- lengths: int32 [32], P('dp'), may hold values from 1024 to 2048, as said below
- pages: int32 [32, 8, 64], P('dp', 'head'), may hold values from 0 to 127, as said below
- w_out: bfloat16 [4096, 4096], P('head', 'dp'), may hold values from -0.75 to 0.75
- norm_gain: float32 [4096], P('head'), may hold values from 0.5 to 1.5
- expert_ids: int32 [32, 2], P('dp'), may hold values from 0 to 7, all different within a row; in each aligned block of 4 rows (0 to 3, 4 to 7, ...) at most 2 rows name the same one
- gate_weights: float32 [32, 2], P('dp'), may hold values from 0.1 to 1
- w_in: bfloat16 [8, 2, 4096, 7168], P('dp', None, None, 'head'), may hold values from -0.09375 to 0.09375
- w_down: bfloat16 [8, 7168, 4096], P('dp', 'head'), may hold values from -0.0625 to 0.0625
Outputs:
- layer_out: bfloat16 [32, 4096], P('dp', 'head')
The draws below stay inside these ranges and needn't reach their ends.
Inputs may be any that keep to these rules, and one draw needn't show every extreme that they name: `lengths`: each request's length; some request has exactly 2048 and some exactly 1024. `pages`: for each request and key head, 64 distinct page numbers, all below ceil(length / 16), always including the page that holds the request's last cached token; in no fixed order. `expert_ids`: per token 2 distinct experts; among the 4 tokens of one dp index no expert is named more than 2 times.
All inputs are finite; a program needn't handle non-finite values.
Results may differ from the reference program's by a relative error of at most 0.012.
Values may be sent and summed in bfloat16 or wider, within the bound.
A program may use at most 128 MiB of HBM per device.

```python
import math
import jax
import jax.numpy as jnp
import numpy as np
from jax import lax

D = 4096
HEADS = 32
KV_HEADS = 8
HD = 128
EXPERTS = 8
TOP = 2
FF = 7168
PAGE = 16
SEL = 64
B_DEV = 4
LEN = 2048
BATCH = 32
PAGES = 128
GROUP = 1
MOST = 2


def draw_query(key, part):
    shape = (BATCH, HEADS, HD)
    base = jax.random.truncated_normal(jax.random.fold_in(key, 1), -4.5, 4.5, shape, jnp.float32)
    return base.astype(jnp.bfloat16)


def draw_fresh_token_keys(key, part):
    shape = (BATCH, KV_HEADS, HD)
    base = 2.0 * jax.random.truncated_normal(jax.random.fold_in(key, 2), -2.25, 2.25, shape, jnp.float32)
    return base.astype(jnp.bfloat16)


def page_plan(key):
    plan_key = jax.random.fold_in(key, 11)
    length_key, end_key, shift_key, score_key = jax.random.split(plan_key, 4)
    lengths = jax.random.randint(length_key, (BATCH,), SEL * PAGE, LEN + 1, dtype=jnp.int32)
    first_end = jax.random.randint(end_key, (), 0, BATCH, dtype=jnp.int32)
    offset_scores = jax.random.randint(shift_key, (), 0, BATCH - 1, dtype=jnp.int32)
    second_end = (first_end + 1 + offset_scores) % BATCH
    lengths = lengths.at[first_end].set(LEN).at[second_end].set(SEL * PAGE)
    used_pages = (lengths + PAGE - 1) // PAGE
    page_num = jnp.arange(PAGES, dtype=jnp.int32)[None, None, :]
    scores = jax.random.randint(score_key, (BATCH, KV_HEADS, PAGES), 0, 1 << 20, dtype=jnp.int32) * PAGES + page_num
    scores = jnp.where(page_num == used_pages[:, None, None] - 1, 1 << 30, scores)
    scores = jnp.where(page_num >= used_pages[:, None, None], -1, scores)
    chosen = jax.lax.top_k(scores, SEL)[1].astype(jnp.int32)
    return (lengths, chosen)


def draw_lengths(key, part):
    return page_plan(key)[0]


def draw_pages(key, part):
    return page_plan(key)[1]


def steps_of(own_key, shape, cuts, low, top_value):
    gain, own = 1.0, jax.random.fold_in(own_key, 6)
    for dim, parts in cuts:
        steps = jnp.exp(jax.random.uniform(jax.random.fold_in(own, dim), (parts,), jnp.float32, low / len(cuts), top_value / len(cuts)))
        gain = gain * jnp.repeat(steps, shape[dim] // parts).reshape([-1 if axis == dim else 1 for axis in range(len(shape))])
    return gain


def deal_out(rng, own, number, rows, amount, top, reach, skew):
    sequence = jax.random.permutation(rng, amount)
    packed, usual = shares(amount, rows * top, reach, skew, True), shares(amount, rows * top, reach, skew, False)
    places = jnp.arange(amount)

    def named(sizes, offset_by):
        used = int((sizes > 0).sum())
        fixed = max(1, used // 4)
        passed = fixed + (places - fixed + offset_by * (used - fixed)) % max(1, amount - fixed)
        return jnp.zeros((amount,), jnp.int32).at[sequence[jnp.where(places < fixed, places, passed)]].set(jnp.asarray(sizes, jnp.int32))

    sizes = jnp.where(number % 4 == 0, named(packed, number // 4), named(usual, number - number // 4 - 1))
    mixed = jax.random.permutation(jax.random.fold_in(own, 3), amount)
    source_of, taker = mixed[0:amount // 2 * 2:2], mixed[1:amount // 2 * 2:2]
    margin = jnp.minimum(sizes[source_of] - 1, reach - sizes[taker]) // 2
    margin = jnp.where((source_of == sequence[0]) | (taker == sequence[0]) | (sizes[taker] == 0), 0, jnp.maximum(margin, 0))
    passed = jax.random.randint(jax.random.fold_in(own, 4), (amount // 2,), 0, 1 << 20) % (margin + 1)
    sizes = sizes.at[source_of].add(-passed).at[taker].add(passed)
    items = jnp.searchsorted(jnp.cumsum(sizes), jnp.arange(rows * top), side="right").astype(jnp.int32)
    listing = items.reshape(top, rows).T
    listing = listing[jax.random.permutation(jax.random.fold_in(own, 1), rows)]
    offset_by = jax.random.randint(jax.random.fold_in(own, 2), (rows, 1), 0, top)
    return jnp.take_along_axis(listing, (jnp.arange(top)[None, :] + offset_by) % top, axis=1)


def shares(count, total, reach, slope, full):
    weights = [(1 << 20) // math.isqrt(rank ** slope) + 1 for rank in range(1, count + 1)]
    largest = reach if full else min(reach, max(-(-total // count), total * weights[0] // sum(weights)))
    least = 1 if total - largest >= count - 1 else 0
    given, surplus = [largest] + [least] * (count - 1), total - largest - least * (count - 1)
    while surplus > 0:
        free = [i for i in range(1, count) if given[i] < largest] or [i for i in range(1, count) if given[i] < reach]
        whole, remaining = sum([weights[i] for i in free]), surplus
        for i in free:
            addition = min(reach - given[i], max(1, remaining * weights[i] // whole), surplus)
            given[i] = given[i] + addition
            surplus = surplus - addition
    return np.array(given)


def noise(key, shape, spread, bound, cuts=(), held_as=jnp.bfloat16):
    drawn = spread * jax.random.normal(key, shape, jnp.float32)
    if cuts:
        drawn = drawn * steps_of(key, shape, cuts, -0.22, 0.18)
    return jnp.clip(drawn, -bound, bound).astype(held_as)


def setup_inputs(seed: int = 0) -> dict:
    key_list = jax.random.split(jax.random.key(seed), 15)
    residual = noise(key_list[0], (BATCH, D), 1.0, 6.0, ((0, 8), (1, 4)))
    query = draw_query(jax.random.fold_in(key_list[14], 71), 0)
    fresh_token_keys = draw_fresh_token_keys(jax.random.fold_in(key_list[14], 71), 0)
    value_new = noise(key_list[3], (BATCH, KV_HEADS, HD), 4.0, 24.0, ((0, 8), (1, 4)))
    key_cache = noise(key_list[4], (BATCH, KV_HEADS, LEN, HD), 1.0, 6.0, ((0, 8), (1, 4)))
    value_cache = noise(key_list[5], (BATCH, KV_HEADS, LEN, HD), 1.0, 6.0, ((0, 8), (1, 4)))
    lengths = draw_lengths(jax.random.fold_in(key_list[14], 71), 0)
    pages = draw_pages(jax.random.fold_in(key_list[14], 71), 0)
    w_out = noise(key_list[8], (HEADS * HD, D), 64 ** -0.5, 0.75, ((0, 4), (1, 8)))
    norm_gain = jnp.clip(1.0 + 0.1 * jax.random.normal(key_list[9], (D,), jnp.float32), 0.5, 1.5)
    expert_ids_keys = jax.random.split(jax.random.fold_in(key_list[10], 1), BATCH // B_DEV)
    expert_ids_turns = jax.random.permutation(jax.random.fold_in(key_list[10], 3), BATCH // B_DEV)
    expert_ids = jax.vmap(lambda own, number: deal_out(jax.random.fold_in(key_list[10], 2), own, number, B_DEV, EXPERTS, TOP, MOST, 2))(expert_ids_keys, expert_ids_turns).reshape((BATCH, TOP))
    gate_weights = jnp.clip(0.1 + 0.9 * jax.random.uniform(key_list[11], (BATCH, TOP), jnp.float32) ** steps_of(key_list[11], (BATCH, TOP), ((0, 8),), -0.2, 0.2), 0.1, 1.0)
    w_in = noise(key_list[12], (EXPERTS * GROUP, 2, D, FF // GROUP), D ** -0.5, 0.09375, ((0, 8), (3, 4)))
    w_down = noise(key_list[13], (EXPERTS * GROUP, FF // GROUP, D), FF ** -0.5, 0.0625, ((0, 8), (1, 4)))
    return {"residual": residual, "query": query, "fresh_token_keys": fresh_token_keys, "value_new": value_new, "key_cache": key_cache, "value_cache": value_cache, "lengths": lengths, "pages": pages, "w_out": w_out, "norm_gain": norm_gain, "expert_ids": expert_ids, "gate_weights": gate_weights, "w_in": w_in, "w_down": w_down}


EPSILON = 1e-05

def attend(request):
    query, fresh_token_keys, value_new, key_cache, value_cache, length, page_list = request
    offsets = jnp.arange(PAGE, dtype=jnp.int32)
    positions = (page_list[:, :, None] * PAGE + offsets[None, None, :]).reshape(KV_HEADS, SEL * PAGE).astype(jnp.int32)
    sel_keys = jnp.take_along_axis(key_cache, positions[:, :, None], axis=1).astype(jnp.float32)
    sel_values = jnp.take_along_axis(value_cache, positions[:, :, None], axis=1).astype(jnp.float32)
    grouped_rows = query.reshape(KV_HEADS, HEADS // KV_HEADS, HD).astype(jnp.float32)
    score_scale = HD ** (-0.5)
    scores = jnp.einsum('kgd,ksd->kgs', grouped_rows, sel_keys) * score_scale
    own_score = jnp.einsum('kgd,kd->kg', grouped_rows, fresh_token_keys.astype(jnp.float32)) * score_scale
    in_range = (positions < length)[:, None, :]
    masked = jnp.where(in_range, scores, -1e+30)
    row_top = jnp.maximum(lax.optimization_barrier(jnp.max(masked, axis=-1)), own_score)
    expo = jnp.where(in_range, jnp.exp(scores - row_top[..., None]), 0.0)
    own_expo = jnp.exp(own_score - row_top)
    denominator = lax.optimization_barrier(jnp.sum(expo, axis=-1)) + own_expo
    weights = (expo / denominator[..., None]).astype(jnp.bfloat16)
    own_weight = (own_expo / denominator).astype(jnp.bfloat16)
    attended = jnp.einsum('kgs,ksd->kgd', weights.astype(jnp.float32), sel_values)
    attended = attended + own_weight.astype(jnp.float32)[..., None] * value_new.astype(jnp.float32)[:, None, :]
    return attended.reshape(HEADS * HD).astype(jnp.bfloat16)

def reference(residual, query, fresh_token_keys, value_new, key_cache, value_cache, lengths, pages, w_out, norm_gain, expert_ids, gate_weights, w_in, w_down):
    attn_rows = lax.map(attend, (query, fresh_token_keys, value_new, key_cache, value_cache, lengths, pages))
    stream = residual.astype(jnp.float32) + jnp.dot(attn_rows, w_out, preferred_element_type=jnp.float32)
    square_mean_value = lax.optimization_barrier(jnp.mean(stream * stream, axis=-1))
    normed = (stream * lax.rsqrt(square_mean_value + EPSILON)[:, None] * norm_gain[None, :]).astype(jnp.bfloat16)
    expert_range = jnp.arange(EXPERTS, dtype=jnp.int32)
    weight_factor = lax.optimization_barrier(jnp.sum(jnp.where(expert_ids[:, :, None] == expert_range[None, None, :], gate_weights[:, :, None], 0.0), axis=1))

    def add_expert(carry, expert):
        expert_out = jnp.zeros((BATCH, D), jnp.float32)
        for slab_part in range(GROUP):
            slab = (expert * GROUP + slab_part).astype(jnp.int32)
            pair = lax.dynamic_index_in_dim(w_in, slab, 0, keepdims=False)
            gate_act = jnp.dot(normed, pair[0], preferred_element_type=jnp.float32)
            up_act = jnp.dot(normed, pair[1], preferred_element_type=jnp.float32)
            hidden = (jax.nn.silu(gate_act) * up_act).astype(jnp.bfloat16)
            down = lax.dynamic_index_in_dim(w_down, slab, 0, keepdims=False)
            expert_out = expert_out + jnp.dot(hidden, down, preferred_element_type=jnp.float32)
        column = lax.dynamic_index_in_dim(weight_factor, expert, 1, keepdims=False)
        return (carry + column[:, None] * expert_out, None)
    mixture, unused = lax.scan(add_expert, jnp.zeros((BATCH, D), jnp.float32), expert_range)
    return (stream + mixture).astype(jnp.bfloat16)
```

```python
import functools

import jax
import jax.numpy as jnp
from jax import lax
from jax.experimental import pallas as pl
from jax.experimental.pallas import tpu as pltpu
from jax.sharding import PartitionSpec as P

EXPERTS = 8
PAGE = 16
EPSILON = 1e-05
LANES = 128
TILE = 256
MESH = pl.DeviceIdType.MESH


def hidden_tile(width):
    return TILE if width % TILE == 0 else width


def layer_kernel(
    nd,
    nh,
    residual_ref,
    query_ref,
    fresh_ref,
    value_new_ref,
    lengths_ref,
    pages_ref,
    gain_ref,
    ids_ref,
    gates_ref,
    key_hbm,
    value_hbm,
    w_out_hbm,
    w_in_hbm,
    w_down_hbm,
    out_ref,
    keys,
    values,
    w_out,
    w_in,
    w_down,
    attn,
    residual_all,
    routing_all,
    rows_all,
    gain_all,
    partial_all,
    stream_all,
    lhs,
    block,
    routing,
    normed,
    hidden,
    slab_send,
    slab_recv,
    total,
    own_stream,
    back_send,
    back_recv,
    cache_sem,
    w_out_sem,
    w_in_sem,
    w_down_sem,
    dp_send,
    dp_recv,
    head_send,
    head_recv,
):
    d, h = lax.axis_index("dp"), lax.axis_index("head")
    rows, heads, head_dim = query_ref.shape
    kv = key_hbm.shape[1]
    cache_len = key_hbm.shape[2]
    members = heads // kv
    tokens = nd * rows
    per_head = residual_ref.shape[1]
    per_dp = w_out.shape[1]
    width = w_down_hbm.shape[2]
    tiles, _, _, tile = w_in.shape
    experts_per = nd // EXPERTS
    page_total = cache_len // PAGE

    cache_copies = []
    for b in range(rows):
        pair = (
            pltpu.make_async_copy(key_hbm.at[b], keys.at[b], cache_sem.at[0, b]),
            pltpu.make_async_copy(value_hbm.at[b], values.at[b], cache_sem.at[1, b]),
        )
        pair[0].start()
        pair[1].start()
        cache_copies.append(pair)
    w_out_copy = pltpu.make_async_copy(w_out_hbm, w_out, w_out_sem)
    w_out_copy.start()

    def w_in_copy(n):
        start = n * tile if isinstance(n, int) else pl.multiple_of(n * tile, tile)
        return pltpu.make_async_copy(
            w_in_hbm.at[0, :, :, pl.ds(start, tile)], w_in.at[n], w_in_sem.at[n]
        )

    for n in range(tiles):
        w_in_copy(n).start()
    down_copies = []
    for k in range(nh):
        owner = lax.rem(h + (k + 1) % nh, nh)
        copy = pltpu.make_async_copy(
            w_down_hbm.at[0, :, pl.ds(pl.multiple_of(owner * per_head, LANES), per_head)],
            w_down.at[k],
            w_down_sem.at[k],
        )
        copy.start()
        down_copies.append(copy)

    def dp_peer(r):
        return (lax.rem(d + r, nd), h)

    def head_peer(r):
        return (d, lax.rem(h + r, nh))

    barrier = pltpu.get_barrier_semaphore()
    for r in range(1, nd):
        pl.semaphore_signal(barrier, inc=1, device_id=dp_peer(r), device_id_type=MESH)
    for r in range(1, nh):
        pl.semaphore_signal(barrier, inc=1, device_id=head_peer(r), device_id_type=MESH)

    lane = lax.broadcasted_iota(jnp.int32, (rows, LANES), 1)
    mine = jnp.zeros((rows, LANES), jnp.float32)
    for j in range(ids_ref.shape[1]):
        mine = mine + jnp.where(ids_ref[:, j : j + 1] == lane, gates_ref[:, j : j + 1], 0.0)
    routing_all[d] = mine
    residual_all[d] = residual_ref[...]
    gain_all[h] = gain_ref[...]

    pl.semaphore_wait(barrier, nd + nh - 2)

    pending = []

    def over_dp(stage, source, target):
        copies = []
        for r in range(1, nd):
            copy = pltpu.make_async_remote_copy(
                src_ref=source(r),
                dst_ref=target,
                send_sem=dp_send.at[stage, r],
                recv_sem=dp_recv.at[stage, r],
                device_id=dp_peer(r),
                device_id_type=MESH,
            )
            copy.start()
            copies.append(copy)
        pending.extend(copies)
        return copies

    def to_head(stage, r, source, target):
        copy = pltpu.make_async_remote_copy(
            src_ref=source,
            dst_ref=target,
            send_sem=head_send.at[stage, r],
            recv_sem=head_recv.at[stage, r],
            device_id=head_peer(r),
            device_id_type=MESH,
        )
        copy.start()
        pending.append(copy)
        return copy

    def arrived(copies):
        for copy in copies:
            copy.wait_recv()

    residual_copies = over_dp(0, lambda r: residual_ref, residual_all.at[d])
    routing_copies = over_dp(1, lambda r: routing_all.at[d], routing_all.at[d])
    gain_copies = [to_head(0, r, gain_ref, gain_all.at[h]) for r in range(1, nh)]

    group_of_row = lax.broadcasted_iota(jnp.int32, (heads, 1), 0) // members

    def by_group(parts):
        chosen = parts[0]
        for k in range(1, kv):
            chosen = jnp.where(group_of_row == k, parts[k], chosen)
        return chosen

    position = lax.broadcasted_iota(jnp.int32, (1, cache_len), 1)
    spread = (
        lax.broadcasted_iota(jnp.int32, (page_total, cache_len), 1) // PAGE
        == lax.broadcasted_iota(jnp.int32, (page_total, cache_len), 0)
    )
    spread = jnp.where(spread, 1.0, 0.0).astype(jnp.bfloat16)
    scale = head_dim ** (-0.5)
    page_shape = (kv, pages_ref.shape[2], page_total)
    page_number = lax.broadcasted_iota(jnp.int32, page_shape, 2)
    for b in range(rows):
        named = jnp.where(pages_ref[b][:, :, None] == page_number, 1.0, 0.0)
        named = jnp.max(named, axis=1)
        named = by_group([named[k : k + 1, :] for k in range(kv)])
        named = jnp.broadcast_to(named, (heads, page_total)).astype(jnp.bfloat16)
        chosen = jnp.dot(named, spread, preferred_element_type=jnp.float32)
        live = (chosen > 0.5) & (position < lengths_ref[b])
        q = query_ref[b]
        fresh = fresh_ref[b].astype(jnp.float32)
        fresh = by_group([fresh[k : k + 1, :] for k in range(kv)])
        own = jnp.sum(q.astype(jnp.float32) * fresh, axis=1, keepdims=True) * scale
        cache_copies[b][0].wait()
        score = by_group(
            [
                lax.dot_general(
                    q,
                    keys[b, k],
                    (((1,), (1,)), ((), ())),
                    preferred_element_type=jnp.float32,
                )
                for k in range(kv)
            ]
        )
        score = jnp.where(live, score * scale, -1e30)
        top = jnp.maximum(jnp.max(score, axis=1, keepdims=True), own)
        expo = jnp.where(live, jnp.exp(score - top), 0.0)
        own_expo = jnp.exp(own - top)
        inverse = 1.0 / (jnp.sum(expo, axis=1, keepdims=True) + own_expo)
        weights = (expo * inverse).astype(jnp.bfloat16)
        own_weight = (own_expo * inverse).astype(jnp.bfloat16).astype(jnp.float32)
        cache_copies[b][1].wait()
        mixed = by_group(
            [
                jnp.dot(weights, values[b, k], preferred_element_type=jnp.float32)
                for k in range(kv)
            ]
        )
        newest = value_new_ref[b].astype(jnp.float32)
        newest = by_group([newest[k : k + 1, :] for k in range(kv)])
        attn[b * heads : (b + 1) * heads, :] = mixed + own_weight * newest

    for x in range(heads):
        rows_all[d, :, x * head_dim : (x + 1) * head_dim] = attn[pl.ds(x, rows, stride=heads), :]
    rows_copies = over_dp(2, lambda r: rows_all.at[d], rows_all.at[d])

    arrived(residual_copies)
    first = d * per_dp
    offset = pl.multiple_of(lax.rem(first, per_head), LANES)
    holds = jnp.where(first // per_head == h, 1.0, 0.0)
    for i in range(nd):
        piece = residual_all[i, :, pl.ds(offset, per_dp)].astype(jnp.float32)
        block[i * rows : (i + 1) * rows, :] = piece * holds

    w_out_copy.wait()
    arrived(rows_copies)
    for i in range(nd):
        lhs[i * rows : (i + 1) * rows, :] = rows_all[i]
    partial = block[...] + jnp.dot(
        lhs[...].astype(jnp.bfloat16), w_out[...], preferred_element_type=jnp.float32
    )
    partial_all[h] = partial.astype(jnp.bfloat16)
    partial_copies = [
        to_head(1, r, partial_all.at[h], partial_all.at[h]) for r in range(1, nh)
    ]
    arrived(partial_copies)
    stream = partial_all[0].astype(jnp.float32)
    for i in range(1, nh):
        stream = stream + partial_all[i].astype(jnp.float32)
    stream_all[d] = stream.astype(jnp.bfloat16)
    stream_copies = over_dp(3, lambda r: stream_all.at[d], stream_all.at[d])

    arrived(routing_copies)
    for i in range(nd):
        routing[i * rows : (i + 1) * rows, :] = routing_all[i]
    lane = lax.broadcasted_iota(jnp.int32, (tokens, LANES), 1)
    weight = jnp.sum(
        jnp.where(lane == d // experts_per, routing[...], 0.0), axis=1, keepdims=True
    )
    arrived(gain_copies)

    arrived(stream_copies)
    squares = jnp.zeros((tokens, 1), jnp.float32)
    for i in range(nd):
        piece = stream_all[i].astype(jnp.float32)
        squares = squares + jnp.sum(piece * piece, axis=1, keepdims=True)
    factor = lax.rsqrt(squares / width + EPSILON)
    for i in range(nd):
        start = i * per_dp
        at = start % per_head
        gain = gain_all[start // per_head, :, at : at + per_dp]
        piece = stream_all[i].astype(jnp.float32) * factor * gain
        normed[:, start : start + per_dp] = piece.astype(jnp.bfloat16)

    def hidden_step(n):
        w_in_copy(n).wait()
        gate_act = jnp.dot(normed[...], w_in[n, 0], preferred_element_type=jnp.float32)
        up_act = jnp.dot(normed[...], w_in[n, 1], preferred_element_type=jnp.float32)
        start = 0 if tiles == 1 else pl.multiple_of(n * tile, tile)
        act = gate_act * jax.nn.sigmoid(gate_act) * up_act
        hidden[:, pl.ds(start, tile)] = act.astype(jnp.bfloat16)

    if tiles == 1:
        hidden_step(0)
    else:
        pl.loop(0, tiles)(hidden_step)

    slab_copies = []
    for k in range(nh):
        down_copies[k].wait()

        @pl.loop(0, per_head // TILE)
        def _(c, k=k):
            columns = pl.ds(pl.multiple_of(c * TILE, TILE), TILE)
            piece = weight * jnp.dot(
                hidden[...], w_down[k, :, columns], preferred_element_type=jnp.float32
            )
            if k < nh - 1:
                slab_send[k, :, columns] = piece.astype(jnp.bfloat16)
            else:
                total[:, columns] = piece

        if k < nh - 1:
            slab_copies.append(to_head(2, k + 1, slab_send.at[k], slab_recv.at[k]))

    for j in range(per_head // per_dp):
        piece = stream_all[h * (per_head // per_dp) + j].astype(jnp.float32)
        for i in range(nd):
            own_stream[i, :, j * per_dp : (j + 1) * per_dp] = piece[i * rows : (i + 1) * rows, :]

    arrived(slab_copies)
    summed = total[...]
    for k in range(nh - 1):
        summed = summed + slab_recv[k].astype(jnp.float32)
    for i in range(nd):
        back_send[i] = summed[i * rows : (i + 1) * rows, :]
    back_copies = over_dp(4, lambda r: back_send.at[lax.rem(d + r, nd)], back_recv.at[d])
    result = own_stream[d] + back_send[d]
    arrived(back_copies)
    for r in range(1, nd):
        result = result + back_recv[lax.rem(d + nd - r, nd)]
    out_ref[...] = result.astype(out_ref.dtype)
    for copy in pending:
        copy.wait_send()


def shards(
    nd,
    nh,
    residual,
    query,
    fresh_token_keys,
    value_new,
    key_cache,
    value_cache,
    lengths,
    pages,
    w_out,
    norm_gain,
    expert_ids,
    gate_weights,
    w_in,
    w_down,
):
    rows, heads, head_dim = query.shape
    per_head = residual.shape[1]
    per_dp = w_out.shape[1]
    tokens = nd * rows
    deep, units = w_in.shape[2], w_in.shape[3]
    tile = hidden_tile(units)
    f32, bf16 = jnp.float32, jnp.bfloat16
    vmem = pl.BlockSpec(memory_space=pltpu.VMEM)
    smem = pl.BlockSpec(memory_space=pltpu.SMEM)
    hbm = pl.BlockSpec(memory_space=pl.ANY)
    scratch = [
        pltpu.VMEM(key_cache.shape, bf16),
        pltpu.VMEM(value_cache.shape, bf16),
        pltpu.VMEM(w_out.shape, bf16),
        pltpu.VMEM((units // tile, 2, deep, tile), bf16),
        pltpu.VMEM((nh, units, per_head), bf16),
        pltpu.VMEM((rows * heads, head_dim), f32),
        pltpu.VMEM((nd, rows, per_head), bf16),
        pltpu.VMEM((nd, rows, LANES), f32),
        pltpu.VMEM((nd, rows, heads * head_dim), f32),
        pltpu.VMEM((nh, 1, per_head), f32),
        pltpu.VMEM((nh, tokens, per_dp), bf16),
        pltpu.VMEM((nd, tokens, per_dp), bf16),
        pltpu.VMEM((tokens, heads * head_dim), f32),
        pltpu.VMEM((tokens, per_dp), f32),
        pltpu.VMEM((tokens, LANES), f32),
        pltpu.VMEM((tokens, deep), bf16),
        pltpu.VMEM((tokens, units), bf16),
        pltpu.VMEM((nh - 1, tokens, per_head), bf16),
        pltpu.VMEM((nh - 1, tokens, per_head), bf16),
        pltpu.VMEM((tokens, per_head), f32),
        pltpu.VMEM((nd, rows, per_head), f32),
        pltpu.VMEM((nd, rows, per_head), f32),
        pltpu.VMEM((nd, rows, per_head), f32),
        pltpu.SemaphoreType.DMA((2, rows)),
        pltpu.SemaphoreType.DMA,
        pltpu.SemaphoreType.DMA((units // tile,)),
        pltpu.SemaphoreType.DMA((nh,)),
        pltpu.SemaphoreType.DMA((5, nd)),
        pltpu.SemaphoreType.DMA((5, nd)),
        pltpu.SemaphoreType.DMA((3, nh)),
        pltpu.SemaphoreType.DMA((3, nh)),
    ]
    return pl.pallas_call(
        functools.partial(layer_kernel, nd, nh),
        out_shape=jax.ShapeDtypeStruct(residual.shape, bf16),
        in_specs=[vmem] * 4 + [smem] + [vmem] * 4 + [hbm] * 5,
        out_specs=vmem,
        scratch_shapes=scratch,
        compiler_params=pltpu.CompilerParams(
            collective_id=0, has_side_effects=True, vmem_limit_bytes=65_000_000
        ),
    )(
        residual,
        query,
        fresh_token_keys,
        value_new,
        lengths,
        pages,
        norm_gain.reshape(1, -1),
        expert_ids,
        gate_weights,
        key_cache,
        value_cache,
        w_out,
        w_in,
        w_down,
    )


def solution(mesh):
    in_specs = (
        P("dp", "head"),
        P("dp", "head", None),
        P("dp", "head", None),
        P("dp", "head", None),
        P("dp", "head", None, None),
        P("dp", "head", None, None),
        P("dp"),
        P("dp", "head", None),
        P("head", "dp"),
        P("head"),
        P("dp", None),
        P("dp", None),
        P("dp", None, None, "head"),
        P("dp", "head", None),
    )
    body = functools.partial(shards, mesh.shape["dp"], mesh.shape["head"])
    return jax.shard_map(
        body, mesh=mesh, in_specs=in_specs, out_specs=P("dp", "head"), check_vma=False
    )
```

```python
import functools

import jax
import jax.numpy as jnp
from jax import lax
from jax.experimental import pallas as pl
from jax.experimental.pallas import tpu as pltpu
from jax.sharding import PartitionSpec as P

EXPERTS = 8
PAGE = 16
EPSILON = 1e-05
LANES = 128
TILE = 256
MESH = pl.DeviceIdType.MESH


def hidden_tile(width):
    return TILE if width % TILE == 0 else width


def layer_kernel(
    nd,
    nh,
    residual_ref,
    query_ref,
    fresh_ref,
    value_new_ref,
    lengths_ref,
    pages_ref,
    gain_ref,
    ids_ref,
    gates_ref,
    key_hbm,
    value_hbm,
    w_out_hbm,
    w_in_hbm,
    w_down_hbm,
    out_ref,
    keys,
    values,
    w_out,
    w_in,
    w_down,
    attn,
    residual_all,
    routing_all,
    rows_all,
    gain_all,
    partial_send,
    partial_all,
    stream_all,
    lhs,
    block,
    routing,
    normed,
    hidden,
    slab_send,
    slab_recv,
    total,
    own_stream,
    back_send,
    back_recv,
    cache_sem,
    w_out_sem,
    w_in_sem,
    w_down_sem,
    dp_send,
    dp_recv,
    head_send,
    head_recv,
    pair_send,
    pair_recv,
):
    d, h = lax.axis_index("dp"), lax.axis_index("head")
    rows, heads, head_dim = query_ref.shape
    kv = key_hbm.shape[1]
    cache_len = key_hbm.shape[2]
    members = heads // kv
    tokens = nd * rows
    per_head = residual_ref.shape[1]
    per_dp = w_out.shape[1]
    parts, _, _, part = stream_all.shape
    width = w_down_hbm.shape[2]
    tiles, _, _, tile = w_in.shape
    experts_per = nd // EXPERTS
    page_total = cache_len // PAGE

    cache_copies = []
    for b in range(rows):
        pair = (
            pltpu.make_async_copy(key_hbm.at[b], keys.at[b], cache_sem.at[0, b]),
            pltpu.make_async_copy(value_hbm.at[b], values.at[b], cache_sem.at[1, b]),
        )
        pair[0].start()
        pair[1].start()
        cache_copies.append(pair)
    w_out_copy = pltpu.make_async_copy(w_out_hbm, w_out, w_out_sem)
    w_out_copy.start()

    def w_in_copy(n):
        start = n * tile if isinstance(n, int) else pl.multiple_of(n * tile, tile)
        return pltpu.make_async_copy(
            w_in_hbm.at[0, :, :, pl.ds(start, tile)], w_in.at[n], w_in_sem.at[n]
        )

    for n in range(tiles):
        w_in_copy(n).start(priority=1)
    down_copies = []
    for k in range(nh):
        owner = lax.rem(h + (k + 1) % nh, nh)
        copy = pltpu.make_async_copy(
            w_down_hbm.at[0, :, pl.ds(pl.multiple_of(owner * per_head, LANES), per_head)],
            w_down.at[k],
            w_down_sem.at[k],
        )
        copy.start(priority=1)
        down_copies.append(copy)

    def dp_peer(r):
        return (lax.rem(d + r, nd), h)

    def head_peer(r):
        return (d, lax.rem(h + r, nh))

    barrier = pltpu.get_barrier_semaphore()
    for r in range(1, nd):
        pl.semaphore_signal(barrier, inc=1, device_id=dp_peer(r), device_id_type=MESH)
    for r in range(1, nh):
        pl.semaphore_signal(barrier, inc=1, device_id=head_peer(r), device_id_type=MESH)

    lane = lax.broadcasted_iota(jnp.int32, (rows, LANES), 1)
    mine = jnp.zeros((rows, LANES), jnp.float32)
    row = lax.broadcasted_iota(jnp.int32, (rows, LANES), 0)
    for j in range(ids_ref.shape[0]):
        for t in range(rows):
            named = (row == t) & (lane == ids_ref[j, t])
            mine = mine + jnp.where(named, gates_ref[j, t], 0.0)
    routing_all[d] = mine
    residual_all[d] = residual_ref[...]
    gain_all[h] = gain_ref[...]

    pl.semaphore_wait(barrier, nd + nh - 2)

    pending = []

    def over_dp(stage, source, target):
        copies = []
        for r in range(1, nd):
            copy = pltpu.make_async_remote_copy(
                src_ref=source(r),
                dst_ref=target,
                send_sem=dp_send.at[stage, r],
                recv_sem=dp_recv.at[stage, r],
                device_id=dp_peer(r),
                device_id_type=MESH,
            )
            copy.start()
            copies.append(copy)
        pending.extend(copies)
        return copies

    def to_head(stage, r, source, target):
        copy = pltpu.make_async_remote_copy(
            src_ref=source,
            dst_ref=target,
            send_sem=head_send.at[stage, r],
            recv_sem=head_recv.at[stage, r],
            device_id=head_peer(r),
            device_id_type=MESH,
        )
        copy.start()
        pending.append(copy)
        return copy

    def arrived(copies):
        for copy in copies:
            copy.wait_recv()

    residual_copies = over_dp(0, lambda r: residual_ref, residual_all.at[d])
    routing_copies = over_dp(1, lambda r: routing_all.at[d], routing_all.at[d])
    gain_copies = [to_head(0, r, gain_ref, gain_all.at[h]) for r in range(1, nh)]

    group_of_row = lax.broadcasted_iota(jnp.int32, (heads, 1), 0) // members

    def by_group(parts):
        chosen = parts[0]
        for k in range(1, kv):
            chosen = jnp.where(group_of_row == k, parts[k], chosen)
        return chosen

    position = lax.broadcasted_iota(jnp.int32, (1, cache_len), 1)
    spread = (
        lax.broadcasted_iota(jnp.int32, (page_total, cache_len), 1) // PAGE
        == lax.broadcasted_iota(jnp.int32, (page_total, cache_len), 0)
    )
    spread = jnp.where(spread, 1.0, 0.0).astype(jnp.bfloat16)
    scale = head_dim ** (-0.5)
    page_shape = (kv, pages_ref.shape[2], page_total)
    page_number = lax.broadcasted_iota(jnp.int32, page_shape, 2)
    for b in range(rows):
        named = jnp.where(pages_ref[b][:, :, None] == page_number, 1.0, 0.0)
        named = jnp.max(named, axis=1)
        named = by_group([named[k : k + 1, :] for k in range(kv)])
        named = jnp.broadcast_to(named, (heads, page_total)).astype(jnp.bfloat16)
        chosen = jnp.dot(named, spread, preferred_element_type=jnp.float32)
        live = (chosen > 0.5) & (position < lengths_ref[b])
        q = query_ref[b]
        fresh = fresh_ref[b].astype(jnp.float32)
        fresh = by_group([fresh[k : k + 1, :] for k in range(kv)])
        own = jnp.sum(q.astype(jnp.float32) * fresh, axis=1, keepdims=True) * scale
        cache_copies[b][0].wait()
        score = by_group(
            [
                lax.dot_general(
                    q,
                    keys[b, k],
                    (((1,), (1,)), ((), ())),
                    preferred_element_type=jnp.float32,
                )
                for k in range(kv)
            ]
        )
        score = jnp.where(live, score * scale, -1e30)
        top = jnp.maximum(jnp.max(score, axis=1, keepdims=True), own)
        expo = jnp.where(live, jnp.exp(score - top), 0.0)
        own_expo = jnp.exp(own - top)
        inverse = 1.0 / (jnp.sum(expo, axis=1, keepdims=True) + own_expo)
        weights = (expo * inverse).astype(jnp.bfloat16)
        own_weight = (own_expo * inverse).astype(jnp.bfloat16).astype(jnp.float32)
        cache_copies[b][1].wait()
        mixed = by_group(
            [
                jnp.dot(weights, values[b, k], preferred_element_type=jnp.float32)
                for k in range(kv)
            ]
        )
        newest = value_new_ref[b].astype(jnp.float32)
        newest = by_group([newest[k : k + 1, :] for k in range(kv)])
        attn[b * heads : (b + 1) * heads, :] = mixed + own_weight * newest

    for x in range(heads):
        head_rows = attn[pl.ds(x, rows, stride=heads), :]
        rows_all[d, :, x * head_dim : (x + 1) * head_dim] = head_rows.astype(jnp.bfloat16)
    rows_copies = over_dp(2, lambda r: rows_all.at[d], rows_all.at[d])

    arrived(residual_copies)
    first = d * per_dp
    offset = pl.multiple_of(lax.rem(first, per_head), LANES)
    holds = jnp.where(first // per_head == h, 1.0, 0.0)
    for i in range(nd):
        piece = residual_all[i, :, pl.ds(offset, per_dp)].astype(jnp.float32)
        block[i * rows : (i + 1) * rows, :] = piece * holds

    w_out_copy.wait()
    arrived(rows_copies)
    for i in range(nd):
        lhs[i * rows : (i + 1) * rows, :] = rows_all[i].astype(jnp.float32)
    partial = block[...] + jnp.dot(
        lhs[...].astype(jnp.bfloat16), w_out[...], preferred_element_type=jnp.float32
    )
    for c in range(parts):
        partial_send[c] = partial[:, c * part : (c + 1) * part].astype(jnp.bfloat16)
    partial_copies = [
        to_head(1, r, partial_send.at[lax.rem(h + r, parts)], partial_all.at[h])
        for r in range(1, nh)
    ]
    mine_of = lax.rem(h, parts)
    partial_all[h] = partial_send[mine_of]
    arrived(partial_copies)
    stream = partial_all[0].astype(jnp.float32)
    for i in range(1, nh):
        stream = stream + partial_all[i].astype(jnp.float32)
    stream_all[mine_of, d] = stream.astype(jnp.bfloat16)
    stream_copies = over_dp(3, lambda r: stream_all.at[mine_of, d], stream_all.at[mine_of, d])
    partner = h + 1 - 2 * lax.rem(h, 2)

    def forward(r):
        piece = stream_all.at[mine_of, lax.rem(d + nd - r, nd)]
        copy = pltpu.make_async_remote_copy(
            src_ref=piece,
            dst_ref=piece,
            send_sem=pair_send.at[r],
            recv_sem=pair_recv.at[r],
            device_id=(d, partner),
            device_id_type=MESH,
        )
        copy.start()
        pending.append(copy)
        return copy

    pair_copies = [forward(0)] if parts == 2 else []

    arrived(routing_copies)
    for i in range(nd):
        routing[i * rows : (i + 1) * rows, :] = routing_all[i]
    lane = lax.broadcasted_iota(jnp.int32, (tokens, LANES), 1)
    weight = jnp.sum(
        jnp.where(lane == d // experts_per, routing[...], 0.0), axis=1, keepdims=True
    )
    arrived(gain_copies)

    for r in range(1, nd):
        stream_copies[r - 1].wait_recv()
        if parts == 2:
            pair_copies.append(forward(r))
    arrived(pair_copies)
    squares = jnp.zeros((tokens, 1), jnp.float32)
    for i in range(nd):
        for c in range(parts):
            piece = stream_all[c, i].astype(jnp.float32)
            squares = squares + jnp.sum(piece * piece, axis=1, keepdims=True)
    factor = lax.rsqrt(squares / width + EPSILON)
    for i in range(nd * parts):
        start = i * part
        at = start % per_head
        gain = gain_all[start // per_head, :, at : at + part]
        piece = stream_all[i % parts, i // parts].astype(jnp.float32) * factor * gain
        normed[:, start : start + part] = piece.astype(jnp.bfloat16)

    def hidden_step(n):
        w_in_copy(n).wait()
        gate_act = jnp.dot(normed[...], w_in[n, 0], preferred_element_type=jnp.float32)
        up_act = jnp.dot(normed[...], w_in[n, 1], preferred_element_type=jnp.float32)
        start = 0 if tiles == 1 else pl.multiple_of(n * tile, tile)
        act = gate_act * jax.nn.sigmoid(gate_act) * up_act
        hidden[:, pl.ds(start, tile)] = act.astype(jnp.bfloat16)

    if tiles == 1:
        hidden_step(0)
    else:
        pl.loop(0, tiles)(hidden_step)

    slab_copies = []
    for k in range(nh):
        down_copies[k].wait()

        @pl.loop(0, per_head // TILE)
        def _(c, k=k):
            columns = pl.ds(pl.multiple_of(c * TILE, TILE), TILE)
            piece = weight * jnp.dot(
                hidden[...], w_down[k, :, columns], preferred_element_type=jnp.float32
            )
            if k < nh - 1:
                slab_send[k, :, columns] = piece.astype(jnp.bfloat16)
            else:
                total[:, columns] = piece

        if k < nh - 1:
            slab_copies.append(to_head(2, k + 1, slab_send.at[k], slab_recv.at[k]))

    for j in range(per_head // part):
        source = h * (per_head // per_dp) + j // parts
        piece = stream_all[j % parts, source].astype(jnp.float32)
        for i in range(nd):
            own_stream[i, :, j * part : (j + 1) * part] = piece[i * rows : (i + 1) * rows, :]

    arrived(slab_copies)
    summed = total[...]
    for k in range(nh - 1):
        summed = summed + slab_recv[k].astype(jnp.float32)
    for i in range(nd):
        back_send[i] = summed[i * rows : (i + 1) * rows, :].astype(jnp.bfloat16)
    back_copies = over_dp(4, lambda r: back_send.at[lax.rem(d + r, nd)], back_recv.at[d])
    result = own_stream[d] + back_send[d].astype(jnp.float32)
    arrived(back_copies)
    for r in range(1, nd):
        result = result + back_recv[lax.rem(d + nd - r, nd)].astype(jnp.float32)
    out_ref[...] = result.astype(out_ref.dtype)
    for copy in pending:
        copy.wait_send()


def shards(
    nd,
    nh,
    residual,
    query,
    fresh_token_keys,
    value_new,
    key_cache,
    value_cache,
    lengths,
    pages,
    w_out,
    norm_gain,
    expert_ids,
    gate_weights,
    w_in,
    w_down,
):
    rows, heads, head_dim = query.shape
    per_head = residual.shape[1]
    per_dp = w_out.shape[1]
    tokens = nd * rows
    deep, units = w_in.shape[2], w_in.shape[3]
    tile = hidden_tile(units)
    parts = 2 if nh % 2 == 0 and per_dp % (2 * LANES) == 0 else 1
    f32, bf16 = jnp.float32, jnp.bfloat16
    vmem = pl.BlockSpec(memory_space=pltpu.VMEM)
    smem = pl.BlockSpec(memory_space=pltpu.SMEM)
    hbm = pl.BlockSpec(memory_space=pl.ANY)
    scratch = [
        pltpu.VMEM(key_cache.shape, bf16),
        pltpu.VMEM(value_cache.shape, bf16),
        pltpu.VMEM(w_out.shape, bf16),
        pltpu.VMEM((units // tile, 2, deep, tile), bf16),
        pltpu.VMEM((nh, units, per_head), bf16),
        pltpu.VMEM((rows * heads, head_dim), f32),
        pltpu.VMEM((nd, rows, per_head), bf16),
        pltpu.VMEM((nd, rows, LANES), f32),
        pltpu.VMEM((nd, rows, heads * head_dim), bf16),
        pltpu.VMEM((nh, 1, per_head), f32),
        pltpu.VMEM((parts, tokens, per_dp // parts), bf16),
        pltpu.VMEM((nh, tokens, per_dp // parts), bf16),
        pltpu.VMEM((parts, nd, tokens, per_dp // parts), bf16),
        pltpu.VMEM((tokens, heads * head_dim), f32),
        pltpu.VMEM((tokens, per_dp), f32),
        pltpu.VMEM((tokens, LANES), f32),
        pltpu.VMEM((tokens, deep), bf16),
        pltpu.VMEM((tokens, units), bf16),
        pltpu.VMEM((nh - 1, tokens, per_head), bf16),
        pltpu.VMEM((nh - 1, tokens, per_head), bf16),
        pltpu.VMEM((tokens, per_head), f32),
        pltpu.VMEM((nd, rows, per_head), f32),
        pltpu.VMEM((nd, rows, per_head), bf16),
        pltpu.VMEM((nd, rows, per_head), bf16),
        pltpu.SemaphoreType.DMA((2, rows)),
        pltpu.SemaphoreType.DMA,
        pltpu.SemaphoreType.DMA((units // tile,)),
        pltpu.SemaphoreType.DMA((nh,)),
        pltpu.SemaphoreType.DMA((5, nd)),
        pltpu.SemaphoreType.DMA((5, nd)),
        pltpu.SemaphoreType.DMA((3, nh)),
        pltpu.SemaphoreType.DMA((3, nh)),
        pltpu.SemaphoreType.DMA((nd,)),
        pltpu.SemaphoreType.DMA((nd,)),
    ]
    return pl.pallas_call(
        functools.partial(layer_kernel, nd, nh),
        out_shape=jax.ShapeDtypeStruct(residual.shape, bf16),
        in_specs=[vmem] * 4 + [smem] + [vmem] * 2 + [smem] * 2 + [hbm] * 5,
        out_specs=vmem,
        scratch_shapes=scratch,
        compiler_params=pltpu.CompilerParams(
            collective_id=0, has_side_effects=True, vmem_limit_bytes=65_000_000
        ),
    )(
        residual,
        query,
        fresh_token_keys,
        value_new,
        lengths,
        pages,
        norm_gain.reshape(1, -1),
        expert_ids.T,
        gate_weights.T,
        key_cache,
        value_cache,
        w_out,
        w_in,
        w_down,
    )


def solution(mesh):
    in_specs = (
        P("dp", "head"),
        P("dp", "head", None),
        P("dp", "head", None),
        P("dp", "head", None),
        P("dp", "head", None, None),
        P("dp", "head", None, None),
        P("dp"),
        P("dp", "head", None),
        P("head", "dp"),
        P("head"),
        P("dp", None),
        P("dp", None),
        P("dp", None, None, "head"),
        P("dp", "head", None),
    )
    body = functools.partial(shards, mesh.shape["dp"], mesh.shape["head"])
    return jax.shard_map(
        body, mesh=mesh, in_specs=in_specs, out_specs=P("dp", "head"), check_vma=False
    )
```
